32 devices in a mesh: seq: 8 (over z, core), dp: 4 (over y, x).
Axes of the slice: x: 2, y: 2, z: 4, core: 2. Of those that a mesh axis runs over, the one named last changes fastest.
Arguments:
- query_proj: bfloat16 [3072, 2560], P(('dp', 'seq')), parts along dimension 0, may hold values from -4.5 to 4.5
- key_proj: bfloat16 [3072, 2560], P(('dp', 'seq')), parts along dimension 0, may hold values from -4.5 to 4.5
- value_proj: bfloat16 [3072, 2560], P(('dp', 'seq')), parts along dimension 0, may hold values from -16 to 16
- token_rows: int32 [3072], P('dp'), parts along dimension 0, may hold values from 0 to 767, as said below
- key_tiles: int32 [64, 4], P(('dp', 'seq')), parts along dimension 0, may hold values from 0 to 15, as said below
- key_count: int32 [64], P(('dp', 'seq')), parts along dimension 0, may hold values from 1 to 4
Outputs:
- attended: bfloat16 [3072, 2560], P(('dp', 'seq')), parts along dimension 0
The draws below stay inside these ranges and needn't reach their ends.
There are 4 independent parts, one for each index of `dp`. The reference program is written for one: setup_inputs(seed, part) draws one part's arguments, and reference() takes and returns one part's arrays. A program takes and returns all parts, laid end to end along the dimension named above; each array names one. Nothing has to cross between parts.
Inputs may be any that keep to these rules, and one draw needn't show every extreme that they name: token_rows is a permutation; the rows of every aligned block of 96 frame-slab rows go to every aligned block of 96 tile-order rows exactly 96 // 8 times. `key_tiles`: for query tile i the entries m < key_count[i] are distinct, include i, and each lies between 2 * (i // 2 - 2) and 2 * (i // 2 + 2) + 1; later entries equal i.
All inputs are finite; a program needn't handle non-finite values.
Results may differ from the reference program's by a relative error of at most 0.0049.
Values may be sent and summed in bfloat16 or wider, within the bound.
No kernel may reach another device: no remote copies, remote signals or barrier semaphores. Data moves between devices by JAX's collectives and lax.ppermute only.
A program may use at most 64 MiB of HBM per device.

```python
import jax
import jax.numpy as jnp
from jax import lax

HD = 128
HW = 2560
TOK_DEV = 96
TOKENS = 768
KMAX = 4
N_SEQ = 8


def slab_map(key):
    per_peer = TOK_DEV // N_SEQ
    dest_keys = jax.random.split(jax.random.fold_in(key, 11), N_SEQ)
    source_keys = jax.random.split(jax.random.fold_in(key, 12), N_SEQ)
    dest_perm = jax.vmap(lambda subkey: jax.random.permutation(subkey, TOK_DEV))(dest_keys)
    source_perm = jax.vmap(lambda subkey: jax.random.permutation(subkey, TOK_DEV))(source_keys)
    column = jnp.arange(TOK_DEV)
    target = column // per_peer
    within = column % per_peer
    source = jnp.arange(N_SEQ)[:, None]
    dest_rows = target[None, :] * TOK_DEV + dest_perm[target[None, :], source * per_peer + within[None, :]]
    reorder = jnp.argsort(source_perm, axis=1)
    placed = jnp.take_along_axis(dest_rows, reorder, axis=1)
    return placed.reshape(TOKENS).astype(jnp.int32)


def tile_window(key):
    tile_total = 2 * N_SEQ
    query_ids = jnp.arange(tile_total)
    tile_row = query_ids // 2
    tile_time = query_ids % 2
    shifts = jax.random.randint(jax.random.fold_in(key, 21), (tile_total,), -1, 2)
    shifts = jnp.where(query_ids == 2, 0, shifts)
    center = tile_row + shifts
    grid_rows = jnp.stack([center - 1, center, center + 1, center], axis=1)
    grid_times = jnp.stack([tile_time, tile_time, tile_time, 1 - tile_time], axis=1)
    inside = (grid_rows >= 0) & (grid_rows < N_SEQ)
    candidate = grid_rows * 2 + grid_times
    ranking = jax.random.randint(jax.random.fold_in(key, 22), (tile_total, KMAX), 0, 1 << 16) * 8
    ranking = ranking + jnp.arange(KMAX)[None, :] + jnp.where(inside, 0, 1 << 22)
    order = jnp.argsort(ranking, axis=1)
    listed = jnp.take_along_axis(candidate, order, axis=1)
    inside_sorted = jnp.take_along_axis(inside, order, axis=1)
    listed = jnp.where(inside_sorted, listed, query_ids[:, None])
    counts = jnp.sum(inside.astype(jnp.int32), axis=1)
    return (listed.astype(jnp.int32), counts.astype(jnp.int32))


def draw_token_rows(key, part):
    return slab_map(key)


def draw_key_tiles(key, part):
    listed, counts = tile_window(key)
    return listed


def draw_key_count(key, part):
    listed, counts = tile_window(key)
    return counts


def draw_query_proj(key, part):
    base = jnp.clip(jax.random.normal(jax.random.fold_in(key, 41), (TOKENS, HW), jnp.float32), -4.0, 4.0)
    return base.astype(jnp.bfloat16)


def draw_key_proj(key, part):
    base = jnp.clip(jax.random.normal(jax.random.fold_in(key, 42), (TOKENS, HW), jnp.float32), -4.0, 4.0)
    return base.astype(jnp.bfloat16)


def block_levels(stream_key, dims, pieces, smallest, largest):
    level = 1.0
    for dim, parts in pieces:
        heights = jax.random.uniform(jax.random.fold_in(jax.random.fold_in(stream_key, 6), dim), (parts,), jnp.float32, smallest / len(pieces), largest / len(pieces))
        level = level * jnp.repeat(jnp.exp(heights), dims[dim] // parts).reshape((-1,) + (1,) * (len(dims) - 1 - dim))
    return level


def noise(own_key, dims, scale, limit, shards=(), dtype=jnp.bfloat16):
    array = jax.random.normal(own_key, dims, jnp.float32) * scale
    if len(shards) > 0:
        array = block_levels(own_key, dims, shards, -0.22, 0.18) * array
    return jnp.clip(array, min=-limit, max=limit).astype(dtype)


def setup_inputs(seed: int = 0, part: int = 0) -> dict:
    arg_keys = jax.random.split(jax.random.key(seed), 7)
    part_splits = jax.random.split(jax.random.fold_in(arg_keys[6], part), 7)
    query_proj = draw_query_proj(jax.random.fold_in(jax.random.fold_in(arg_keys[6], part), 71), part)
    key_proj = draw_key_proj(jax.random.fold_in(jax.random.fold_in(arg_keys[6], part), 71), part)
    value_proj = noise(part_splits[2], (TOKENS, HW), 4.0, 16.0, ((0, 8),))
    token_rows = draw_token_rows(jax.random.fold_in(jax.random.fold_in(arg_keys[6], part), 71), part)
    key_tiles = draw_key_tiles(jax.random.fold_in(jax.random.fold_in(arg_keys[6], part), 71), part)
    key_count = draw_key_count(jax.random.fold_in(jax.random.fold_in(arg_keys[6], part), 71), part)
    return dict(query_proj=query_proj, key_proj=key_proj, value_proj=value_proj, token_rows=token_rows, key_tiles=key_tiles, key_count=key_count)


def reference(query_proj, key_proj, value_proj, token_rows, key_tiles, key_count):
    inverse = jnp.argsort(token_rows)
    tile_total = key_tiles.shape[0]
    tile_rows = query_proj.shape[0] // tile_total
    feat_width = query_proj.shape[1]
    head_count = feat_width // HD
    query_tiles = query_proj[inverse].reshape(tile_total, tile_rows, feat_width)
    key_rows = key_proj[inverse].reshape(tile_total, tile_rows, feat_width)
    value_rows = value_proj[inverse].reshape(tile_total, tile_rows, feat_width)
    scaling = HD ** -0.5

    def one_tile(operands):
        query_block, tile_ids, tile_count = operands
        key_block = key_rows[tile_ids].reshape(-1, head_count, HD).astype(jnp.float32)
        value_block = value_rows[tile_ids].reshape(-1, head_count, HD).astype(jnp.float32)
        query_heads = query_block.reshape(tile_rows, head_count, HD).astype(jnp.float32)
        scores = jnp.einsum("qhd,khd->hqk", query_heads, key_block) * scaling
        active = jnp.repeat(jnp.arange(KMAX) < tile_count, tile_rows)
        scores = jnp.where(active[None, None, :], scores, -jnp.inf)
        peak = jnp.max(scores, axis=-1, keepdims=True)
        exponent = jnp.exp(scores - peak)
        weights = (exponent / jnp.sum(exponent, axis=-1, keepdims=True)).astype(jnp.bfloat16)
        mixed = jnp.einsum("hqk,khd->qhd", weights.astype(jnp.float32), value_block)
        return mixed.reshape(tile_rows, feat_width).astype(jnp.bfloat16)

    tile_out = lax.map(one_tile, (query_tiles, key_tiles, key_count))
    return tile_out.reshape(-1, feat_width)[token_rows]
```

```python
import functools

import jax
import jax.numpy as jnp
from jax import lax
from jax.experimental import pallas as pl
from jax.experimental.pallas import tpu as pltpu
from jax.sharding import PartitionSpec as P

HD = 128
KMAX = 4
REACH = 2


def passed_along(value, axis, by):
    size = lax.axis_size(axis)
    pairs = [(i, i + by) for i in range(size) if 0 <= i + by < size]
    return lax.ppermute(value, axis, pairs)


def order_for(inverse, owner_dev, rows_dev):
    sources = lax.dynamic_slice_in_dim(inverse, owner_dev * rows_dev, rows_dev) // rows_dev
    keyed = sources * rows_dev + jnp.arange(rows_dev, dtype=jnp.int32)
    return jnp.argsort(keyed)


def attend_heads(query_rows, key_rows, value_rows, allowed, head_count):
    last = query_rows.ndim - 1

    def one_head(head_index):
        start = head_index * HD
        query_head = lax.dynamic_slice_in_dim(query_rows, start, HD, last)
        key_head = lax.dynamic_slice_in_dim(key_rows, start, HD, last)
        value_head = lax.dynamic_slice_in_dim(value_rows, start, HD, last)
        scores = jnp.einsum(
            "...qd,...kd->...qk", query_head, key_head, preferred_element_type=jnp.float32
        ) * HD ** (-0.5)
        scores = jnp.where(allowed, scores, -jnp.inf)
        peak = jnp.max(scores, axis=-1, keepdims=True)
        exponent = jnp.exp(scores - peak)
        weights = (exponent / jnp.sum(exponent, axis=-1, keepdims=True)).astype(jnp.bfloat16)
        mixed = jnp.einsum(
            "...qk,...kd->...qd", weights, value_head, preferred_element_type=jnp.float32
        )
        return mixed.astype(jnp.bfloat16)

    return lax.map(one_head, jnp.arange(head_count))


def shards(query_proj, key_proj, value_proj, token_rows, key_tiles, key_count):
    members = lax.axis_size("seq")
    myself = lax.axis_index("seq")
    rows_dev = query_proj.shape[0]
    feat_width = query_proj.shape[1]
    per_peer = rows_dev // members
    tile_rows = rows_dev // 2
    head_count = feat_width // HD
    inverse = jnp.argsort(token_rows)
    own_dest = lax.dynamic_slice_in_dim(token_rows, myself * rows_dev, rows_dev)
    send_order = jnp.argsort(own_dest)
    sorted_query = query_proj[send_order].reshape(members, per_peer, feat_width)
    sorted_keys = key_proj[send_order].reshape(members, per_peer, feat_width)
    sorted_values = value_proj[send_order].reshape(members, per_peer, feat_width)
    order_own = order_for(inverse, myself, rows_dev)
    placement_own = jnp.argsort(order_own)
    arrived_query, arrived_keys, arrived_values = (
        lax.all_to_all(sorted_query, "seq", split_axis=0, concat_axis=0, tiled=True),
        lax.all_to_all(sorted_keys, "seq", split_axis=0, concat_axis=0, tiled=True),
        lax.all_to_all(sorted_values, "seq", split_axis=0, concat_axis=0, tiled=True),
    )
    query_tile = arrived_query.reshape(rows_dev, feat_width)[placement_own]
    key_tile = arrived_keys.reshape(rows_dev, feat_width)[placement_own]
    value_tile = arrived_values.reshape(rows_dev, feat_width)[placement_own]
    blocks = []
    for offset in range(-REACH, REACH + 1):
        if offset == 0:
            blocks.append((key_tile, value_tile))
        else:
            blocks.append(passed_along((key_tile, value_tile), "seq", -offset))
    window_keys = jnp.concatenate([pair[0] for pair in blocks], axis=0)
    window_values = jnp.concatenate([pair[1] for pair in blocks], axis=0)
    entry_live = jnp.arange(KMAX)[None, :] < key_count[:, None]
    window_ids = (
        (myself + jnp.arange(-REACH, REACH + 1))[:, None] * 2 + jnp.arange(2)[None, :]
    ).reshape(-1)
    matches = (key_tiles[:, :, None] == window_ids[None, None, :]) & entry_live[:, :, None]
    listed = jnp.any(matches, axis=1)
    allowed = jnp.repeat(jnp.repeat(listed, tile_rows, axis=0), tile_rows, axis=1)
    mixed = attend_heads(query_tile, window_keys, window_values, allowed, head_count)
    tile_out = jnp.moveaxis(mixed, 0, -2).reshape(rows_dev, feat_width)
    back_send = tile_out[order_own].reshape(members, per_peer, feat_width)
    arrived_back = lax.all_to_all(back_send, "seq", split_axis=0, concat_axis=0, tiled=True)
    return arrived_back.reshape(rows_dev, feat_width)[jnp.argsort(send_order)]


META = 8
MASKED = -1e30
VMEM = pltpu.VMEM
SMEM = pltpu.SMEM


def whole(space=VMEM):
    return pl.BlockSpec(memory_space=space)


def params():
    return pltpu.CompilerParams(vmem_limit_bytes=16 << 20)


def pack_kv_kernel(group, heads, offs, tiles, count, key_ref, value_ref, *outs):
    rows = key_ref.shape[0]
    row = lax.broadcasted_iota(jnp.int32, (META, HD), 0)
    lane = lax.broadcasted_iota(jnp.int32, (META, HD), 1)
    listed = jnp.zeros((META, HD), jnp.bool_)
    for t in range(tiles.shape[0]):
        for m in range(tiles.shape[1]):
            entry = jnp.where(m < count[t], tiles[t, m], -1)
            listed = listed | ((row == t) & (lane == entry))
    meta = jnp.where(listed, 1.0, 0.0).astype(jnp.bfloat16)
    for j in range(group):
        base = offs[j]
        for h in range(heads):
            cols = pl.ds(pl.multiple_of(base + h * HD, HD), HD)
            outs[j][pl.ds(2 * h * rows, rows), :] = key_ref[:, cols]
            outs[j][pl.ds((2 * h + 1) * rows, rows), :] = value_ref[:, cols]
        outs[j][pl.ds(2 * heads * rows, META), :] = meta


def pack_q_kernel(group, heads, offs, query_ref, *outs):
    for j in range(group):
        base = offs[j]
        for h in range(heads):
            cols = pl.ds(pl.multiple_of(base + h * HD, HD), HD)
            outs[j][h] = query_ref[:, cols]


def attend_kernel(blocks, heads, place_ref, tile_ref, query_ref, *refs):
    kv, out_ref = refs[:blocks], refs[blocks]
    rows = query_ref.shape[1]
    lists = jnp.concatenate([r[pl.ds(2 * heads * rows, META), :] for r in kv], axis=0)
    place = lax.broadcasted_iota(jnp.int32, (blocks * META, rows), 0) == place_ref[...]
    mine = lax.dot_general(
        jnp.where(place, 1.0, 0.0).astype(jnp.bfloat16), lists,
        (((0,), (0,)), ((), ())), preferred_element_type=jnp.float32,
    ).astype(jnp.bfloat16)
    tile = lax.broadcasted_iota(jnp.int32, (HD, blocks * rows), 0) == tile_ref[...]
    allowed = jnp.dot(
        mine, jnp.where(tile, 1.0, 0.0).astype(jnp.bfloat16), preferred_element_type=jnp.float32
    )
    bias = jnp.where(allowed > 0.5, 0.0, MASKED)
    for h in range(heads):
        keys = jnp.concatenate([r[pl.ds(2 * h * rows, rows), :] for r in kv], axis=0)
        values = jnp.concatenate([r[pl.ds((2 * h + 1) * rows, rows), :] for r in kv], axis=0)
        scores = lax.dot_general(
            query_ref[h], keys, (((1,), (1,)), ((), ())), preferred_element_type=jnp.float32
        ) * HD ** (-0.5) + bias
        peak = jnp.max(scores, axis=-1, keepdims=True)
        exponent = jnp.exp(scores - peak)
        total = jnp.sum(exponent, axis=-1, keepdims=True)
        weights = (exponent / total).astype(jnp.bfloat16)
        out_ref[h] = jnp.dot(weights, values, preferred_element_type=jnp.float32).astype(jnp.bfloat16)


def unpack_kernel(group, heads, offs, *refs):
    parts, out_ref = refs[:group], refs[group]
    for j in range(group):
        base = offs[j]
        for h in range(heads):
            cols = pl.ds(pl.multiple_of(base + h * HD, HD), HD)
            out_ref[:, cols] = parts[j][h]


def by_heads(query_proj, key_proj, value_proj, token_rows, key_tiles, key_count):
    members = lax.axis_size("seq")
    chips = members // 2
    myself = lax.axis_index("seq")
    chip, core = myself // 2, myself % 2
    rows, feat = query_proj.shape
    heads = feat // HD // chips
    tiles_dev = key_tiles.shape[0]
    tile_rows = rows // tiles_dev
    bf16 = jnp.bfloat16

    def shifted(value, by):
        pairs = [(2 * c + k, 2 * ((c + by) % chips) + k) for c in range(chips) for k in range(2)]
        return lax.ppermute(value, "seq", pairs)

    def crossed(value):
        return lax.ppermute(value, "seq", [(i, i ^ 1) for i in range(members)])

    steps = list(range(chips))
    offs = jnp.stack([((chip + d) % chips) * heads * HD for d in steps]).astype(jnp.int32)
    kv_shape = jax.ShapeDtypeStruct((2 * heads * rows + META, HD), bf16)
    q_shape = jax.ShapeDtypeStruct((heads, rows, HD), bf16)
    kv_send = pl.pallas_call(
        functools.partial(pack_kv_kernel, chips, heads),
        out_shape=[kv_shape] * chips,
        in_specs=[whole(SMEM)] * 3 + [whole()] * 2,
        out_specs=[whole()] * chips,
        compiler_params=params(),
        name="pack_kv",
    )(offs, key_tiles, key_count, key_proj, value_proj)
    q_send = pl.pallas_call(
        functools.partial(pack_q_kernel, chips, heads),
        out_shape=[q_shape] * chips,
        in_specs=[whole(SMEM), whole()],
        out_specs=[whole()] * chips,
        compiler_params=params(),
        name="pack_q",
    )(offs, query_proj)
    kv_here = [kv_send[0]] + [shifted(kv_send[d], d) for d in steps[1:]]
    q_here = [q_send[0]] + [shifted(q_send[d], d) for d in steps[1:]]
    kv_there = [crossed(value) for value in kv_here]
    kv = kv_here + kv_there

    slab_tiles = (token_rows // tile_rows).reshape(members, rows)
    source_chip = (chip - jnp.arange(chips)) % chips
    source = jnp.concatenate([source_chip * 2 + core, source_chip * 2 + 1 - core])
    block_tiles = slab_tiles[source]
    key_tile = block_tiles.reshape(1, members * rows)
    owner = block_tiles[:chips] // tiles_dev
    place = ((chip - owner // 2) % chips + jnp.where(owner % 2 == core, 0, chips)) * META
    place = place + block_tiles[:chips] % tiles_dev

    attend = pl.pallas_call(
        functools.partial(attend_kernel, members, heads),
        out_shape=q_shape,
        in_specs=[whole()] * (3 + members),
        out_specs=whole(),
        compiler_params=params(),
        name="attend",
        cost_estimate=pl.CostEstimate(
            flops=4 * heads * rows * rows * members * HD,
            bytes_accessed=4 * heads * rows * HD * (members + 1),
            transcendentals=heads * rows * rows * members,
        ),
    )
    outs = [attend(place[d : d + 1], key_tile, q_here[d], *kv) for d in steps]
    back = [outs[0]] + [shifted(outs[d], -d) for d in steps[1:]]
    return pl.pallas_call(
        functools.partial(unpack_kernel, chips, heads),
        out_shape=jax.ShapeDtypeStruct((rows, feat), bf16),
        in_specs=[whole(SMEM)] + [whole()] * chips,
        out_specs=whole(),
        compiler_params=params(),
        name="unpack",
    )(offs, *back)


def shards_of(*args):
    members = lax.axis_size("seq")
    rows, feat = args[0].shape
    chips = members // 2
    tiles = args[4].shape[0]
    if (
        members % 2 == 0
        and feat // HD % chips == 0
        and rows % 16 == 0
        and tiles <= META
        and tiles * members <= HD
    ):
        return by_heads(*args)
    return shards(*args)


def solution(mesh):
    return jax.shard_map(
        shards_of,
        mesh=mesh,
        in_specs=(
            P(("dp", "seq"), None),
            P(("dp", "seq"), None),
            P(("dp", "seq"), None),
            P("dp"),
            P(("dp", "seq"), None),
            P(("dp", "seq")),
        ),
        out_specs=P(("dp", "seq"), None),
        check_vma=False,
    )
```

```python
import functools

import jax
import jax.numpy as jnp
from jax import lax
from jax.experimental import pallas as pl
from jax.experimental.pallas import tpu as pltpu
from jax.sharding import PartitionSpec as P

HD = 128
KMAX = 4
REACH = 2


def passed_along(value, axis, by):
    size = lax.axis_size(axis)
    pairs = [(i, i + by) for i in range(size) if 0 <= i + by < size]
    return lax.ppermute(value, axis, pairs)


def order_for(inverse, owner_dev, rows_dev):
    sources = lax.dynamic_slice_in_dim(inverse, owner_dev * rows_dev, rows_dev) // rows_dev
    keyed = sources * rows_dev + jnp.arange(rows_dev, dtype=jnp.int32)
    return jnp.argsort(keyed)


def attend_heads(query_rows, key_rows, value_rows, allowed, head_count):
    last = query_rows.ndim - 1

    def one_head(head_index):
        start = head_index * HD
        query_head = lax.dynamic_slice_in_dim(query_rows, start, HD, last)
        key_head = lax.dynamic_slice_in_dim(key_rows, start, HD, last)
        value_head = lax.dynamic_slice_in_dim(value_rows, start, HD, last)
        scores = jnp.einsum(
            "...qd,...kd->...qk", query_head, key_head, preferred_element_type=jnp.float32
        ) * HD ** (-0.5)
        scores = jnp.where(allowed, scores, -jnp.inf)
        peak = jnp.max(scores, axis=-1, keepdims=True)
        exponent = jnp.exp(scores - peak)
        weights = (exponent / jnp.sum(exponent, axis=-1, keepdims=True)).astype(jnp.bfloat16)
        mixed = jnp.einsum(
            "...qk,...kd->...qd", weights, value_head, preferred_element_type=jnp.float32
        )
        return mixed.astype(jnp.bfloat16)

    return lax.map(one_head, jnp.arange(head_count))


def shards(query_proj, key_proj, value_proj, token_rows, key_tiles, key_count):
    members = lax.axis_size("seq")
    myself = lax.axis_index("seq")
    rows_dev = query_proj.shape[0]
    feat_width = query_proj.shape[1]
    per_peer = rows_dev // members
    tile_rows = rows_dev // 2
    head_count = feat_width // HD
    inverse = jnp.argsort(token_rows)
    own_dest = lax.dynamic_slice_in_dim(token_rows, myself * rows_dev, rows_dev)
    send_order = jnp.argsort(own_dest)
    sorted_query = query_proj[send_order].reshape(members, per_peer, feat_width)
    sorted_keys = key_proj[send_order].reshape(members, per_peer, feat_width)
    sorted_values = value_proj[send_order].reshape(members, per_peer, feat_width)
    order_own = order_for(inverse, myself, rows_dev)
    placement_own = jnp.argsort(order_own)
    arrived_query, arrived_keys, arrived_values = (
        lax.all_to_all(sorted_query, "seq", split_axis=0, concat_axis=0, tiled=True),
        lax.all_to_all(sorted_keys, "seq", split_axis=0, concat_axis=0, tiled=True),
        lax.all_to_all(sorted_values, "seq", split_axis=0, concat_axis=0, tiled=True),
    )
    query_tile = arrived_query.reshape(rows_dev, feat_width)[placement_own]
    key_tile = arrived_keys.reshape(rows_dev, feat_width)[placement_own]
    value_tile = arrived_values.reshape(rows_dev, feat_width)[placement_own]
    blocks = []
    for offset in range(-REACH, REACH + 1):
        if offset == 0:
            blocks.append((key_tile, value_tile))
        else:
            blocks.append(passed_along((key_tile, value_tile), "seq", -offset))
    window_keys = jnp.concatenate([pair[0] for pair in blocks], axis=0)
    window_values = jnp.concatenate([pair[1] for pair in blocks], axis=0)
    entry_live = jnp.arange(KMAX)[None, :] < key_count[:, None]
    window_ids = (
        (myself + jnp.arange(-REACH, REACH + 1))[:, None] * 2 + jnp.arange(2)[None, :]
    ).reshape(-1)
    matches = (key_tiles[:, :, None] == window_ids[None, None, :]) & entry_live[:, :, None]
    listed = jnp.any(matches, axis=1)
    allowed = jnp.repeat(jnp.repeat(listed, tile_rows, axis=0), tile_rows, axis=1)
    mixed = attend_heads(query_tile, window_keys, window_values, allowed, head_count)
    tile_out = jnp.moveaxis(mixed, 0, -2).reshape(rows_dev, feat_width)
    back_send = tile_out[order_own].reshape(members, per_peer, feat_width)
    arrived_back = lax.all_to_all(back_send, "seq", split_axis=0, concat_axis=0, tiled=True)
    return arrived_back.reshape(rows_dev, feat_width)[jnp.argsort(send_order)]


LATE = 2
META = 8
MASKED = -1e30
LOG2E = 1.4426950408889634
VMEM = pltpu.VMEM
SMEM = pltpu.SMEM


def whole(space=VMEM):
    return pl.BlockSpec(memory_space=space)


def params():
    return pltpu.CompilerParams(vmem_limit_bytes=16 << 20)


@functools.cache
def rounds_of(chips):
    steps = range(1, chips)
    if chips & (chips - 1) == 0:
        rounds = [tuple(c ^ by for c in range(chips)) for by in steps]
    else:
        rounds = [tuple((c + by) % chips for c in range(chips)) for by in steps]

    return tuple(rounds[::-1])


def inverse_of(perm):
    return tuple(perm.index(c) for c in range(len(perm)))


def by_chip(table, chip):
    value = jnp.int32(table[0])
    for c, entry in enumerate(table[1:], 1):
        value = jnp.where(chip == c, entry, value)
    return value


def pack_kernel(dest, heads, parts, tiles_hbm, count_hbm, query_ref, key_ref, value_ref, *refs):
    outs, (tiles, count, sem, small_sem) = refs[:-4], refs[-4:]
    rows = query_ref.shape[0]
    chip = lax.axis_index("seq") // 2
    lists = [
        pltpu.make_async_copy(tiles_hbm, tiles, small_sem),
        pltpu.make_async_copy(count_hbm, count, small_sem),
    ]
    for item in lists:
        item.start()
    copies = []
    for (r, chosen), out in zip(parts, outs):
        base = by_chip(dest[r], chip) * (heads * HD)
        for i, h in enumerate(chosen):
            cols = pl.ds(pl.multiple_of(base + h * HD, HD), HD)
            for j, ref in enumerate((query_ref, key_ref, value_ref)):
                target = out.at[pl.ds((3 * i + j) * rows, rows), :]
                copies.append(pltpu.make_async_copy(ref.at[:, cols], target, sem))
                copies[-1].start()
    for item in lists:
        item.wait()
    row = lax.broadcasted_iota(jnp.int32, (META, HD), 0)
    lane = lax.broadcasted_iota(jnp.int32, (META, HD), 1)
    listed = jnp.zeros((META, HD), jnp.bool_)
    for t in range(tiles.shape[0]):
        for m in range(tiles.shape[1]):
            entry = jnp.where(m < count[t], tiles[t, m], -1)
            listed = listed | ((row == t) & (lane == entry))
    meta = jnp.where(listed, 1.0, 0.0).astype(jnp.bfloat16)
    for (r, chosen), out in zip(parts, outs):
        if 0 in chosen:
            out[pl.ds(3 * len(chosen) * rows, META), :] = meta
    for item in copies:
        item.wait()


def mask_kernel(blocks, heads, place_ref, tile_ref, *refs):
    got, deny_ref, owner_ref = refs[:blocks], refs[blocks], refs[blocks + 1]
    rows = place_ref.shape[1]
    lists = jnp.concatenate([r[pl.ds(3 * heads * rows, META), :] for r in got], axis=0)
    row = lax.broadcasted_iota(jnp.int32, (blocks * META, rows), 0)
    first = (((0,), (0,)), ((), ()))
    for r in range(place_ref.shape[0]):
        place = jnp.where(row == place_ref[pl.ds(r, 1), :], 1.0, 0.0).astype(jnp.bfloat16)
        mine = lax.dot_general(place, lists, first, preferred_element_type=jnp.float32)
        deny_ref[r] = jnp.where(mine > 0.5, 0.0, MASKED).astype(jnp.bfloat16)
    tile = lax.broadcasted_iota(jnp.int32, (HD, tile_ref.shape[1]), 0) == tile_ref[...]
    same = lax.broadcasted_iota(jnp.int32, (HD, HD), 0) == lax.broadcasted_iota(jnp.int32, (HD, HD), 1)
    owner_ref[...] = lax.dot_general(
        jnp.where(tile, 1.0, 0.0).astype(jnp.bfloat16),
        jnp.where(same, 1.0, 0.0).astype(jnp.bfloat16),
        first, preferred_element_type=jnp.float32,
    ).astype(jnp.bfloat16)


def attend_kernel(blocks, index, deny_ref, owner_ref, *refs):
    got, (out_ref, scores_ref, weights_ref) = refs[:blocks], refs[blocks:]
    heads, rows = out_ref.shape[:2]
    deny, owner = deny_ref[index], owner_ref[...]
    ones = jnp.ones((blocks * rows, HD), jnp.bfloat16)

    def joined(part, h, other):
        at = pl.ds((3 * h + part) * rows, rows)
        return jnp.concatenate([jnp.concatenate([r[at, :] for r in got], axis=0), other], axis=1)

    for h in range(heads):
        query = jnp.concatenate([got[index][pl.ds(3 * h * rows, rows), :], deny], axis=1)
        scores_ref[h] = lax.dot_general(
            query, joined(1, h, owner), (((1,), (1,)), ((), ())), preferred_element_type=jnp.float32
        )
    for h in range(heads):
        scores = scores_ref[h]
        peak = jnp.max(scores, axis=-1, keepdims=True)
        weights_ref[h] = jnp.exp2((scores - peak) * (HD ** (-0.5) * LOG2E)).astype(jnp.bfloat16)
    for h in range(heads):
        mixed = jnp.dot(weights_ref[h], joined(2, h, ones), preferred_element_type=jnp.float32)
        out_ref[h] = (mixed[:, :HD] / mixed[:, HD:]).astype(jnp.bfloat16)


def unpack_kernel(dest, heads, chosen, aliased, *refs):
    parts, out_ref, sem = refs[aliased : aliased + len(dest)], refs[-2], refs[-1]
    chip = lax.axis_index("seq") // 2
    copies = []
    for r, part in enumerate(parts):
        base = by_chip(dest[r], chip) * (heads * HD)
        for i, h in enumerate(chosen):
            cols = pl.ds(pl.multiple_of(base + h * HD, HD), HD)
            copies.append(pltpu.make_async_copy(part.at[i], out_ref.at[:, cols], sem))
            copies[-1].start()
    for item in copies:
        item.wait()


def by_heads(query_proj, key_proj, value_proj, token_rows, key_tiles, key_count):
    members = lax.axis_size("seq")
    chips = members // 2
    myself = lax.axis_index("seq")
    chip, core = myself >> 1, myself & 1
    rows, feat = query_proj.shape
    heads = feat // HD // chips
    tiles_dev = key_tiles.shape[0]
    tile_rows = rows // tiles_dev
    bf16 = jnp.bfloat16
    dest = (tuple(range(chips)),) + rounds_of(chips)
    came = tuple(inverse_of(perm) for perm in dest)
    steps = range(chips)
    late = max(0, min(LATE, heads - 1))
    groups = [tuple(range(heads - late))] + ([tuple(range(heads - late, heads))] if late else [])

    def sent(value, perm):
        pairs = [(2 * a + k, 2 * b + k) for a, b in enumerate(perm) for k in range(2)]
        return lax.ppermute(value, "seq", pairs)

    def crossed(value):
        return lax.ppermute(value, "seq", [(i, i ^ 1) for i in range(members)])

    operands = [
        pltpu.with_memory_space_constraint(x, pltpu.HBM)
        for x in (key_tiles, key_count, query_proj, key_proj, value_proj)
    ]

    def pack(parts):
        return pl.pallas_call(
            functools.partial(pack_kernel, dest, heads, parts),
            out_shape=[
                jax.ShapeDtypeStruct((3 * len(chosen) * rows + META * (0 in chosen), HD), bf16)
                for r, chosen in parts
            ],
            in_specs=[whole(pltpu.HBM)] * 5,
            out_specs=[whole()] * len(parts),
            scratch_shapes=[
                SMEM(key_tiles.shape, jnp.int32),
                SMEM(key_count.shape, jnp.int32),
                pltpu.SemaphoreType.DMA,
                pltpu.SemaphoreType.DMA,
            ],
            compiler_params=params(),
        )(*operands)

    parts = [(r, chosen) for chosen in groups for r in (*steps[1:], 0)]
    packed = dict(zip(parts[:1], pack(parts[:1])))
    packed.update(zip(parts[1:], pack(parts[1:])))
    got = []
    for g, chosen in enumerate(groups):
        here = [packed[0, chosen]] + [sent(packed[r, chosen], dest[r]) for r in steps[1:]]
        got.append(here + [crossed(value) for value in here])

    slab_tiles = (token_rows // tile_rows).reshape(members, rows)
    source_chip = jnp.stack([by_chip(table, chip) for table in came])
    source = jnp.concatenate([source_chip * 2 + core, source_chip * 2 + 1 - core])
    block_tiles = slab_tiles[source]
    key_tile = block_tiles.reshape(1, members * rows)
    owner = block_tiles[:chips] // tiles_dev
    arrived = jnp.sum(
        jnp.where(source_chip == (owner >> 1)[..., None], jnp.arange(chips), 0), axis=-1
    )
    place = (arrived + jnp.where((owner & 1) == core, 0, chips)) * META
    place = place + block_tiles[:chips] % tiles_dev
    deny, owned = pl.pallas_call(
        functools.partial(mask_kernel, members, len(groups[0])),
        out_shape=[
            jax.ShapeDtypeStruct((chips, rows, HD), bf16),
            jax.ShapeDtypeStruct((members * rows, HD), bf16),
        ],
        in_specs=[whole()] * (2 + members),
        out_specs=[whole()] * 2,
        compiler_params=params(),
        name="mask",
    )(place, key_tile, *got[0])

    result = None
    for g, chosen in enumerate(groups):
        count = len(chosen)

        def attend(r):
            return pl.pallas_call(
                functools.partial(attend_kernel, members, r),
                out_shape=jax.ShapeDtypeStruct((count, rows, HD), bf16),
                in_specs=[whole()] * (2 + members),
                out_specs=whole(),
                scratch_shapes=[
                    VMEM((count, rows, members * rows), jnp.float32),
                    VMEM((count, rows, members * rows), bf16),
                ],
                compiler_params=params(),
                cost_estimate=pl.CostEstimate(
                    flops=4 * count * rows * rows * members * HD,
                    bytes_accessed=6 * count * rows * HD * members,
                    transcendentals=count * rows * rows * members,
                ),
            )(deny, owned, *got[g])

        outs = [attend(r) for r in steps]
        back = [outs[0]] + [sent(outs[r], came[r]) for r in steps[1:]]
        carried = [] if result is None else [result]
        result = pl.pallas_call(
            functools.partial(unpack_kernel, dest, heads, chosen, len(carried)),
            out_shape=jax.ShapeDtypeStruct((rows, feat), bf16),
            in_specs=[whole(pltpu.HBM)] * len(carried) + [whole()] * chips,
            out_specs=whole(pltpu.HBM),
            scratch_shapes=[pltpu.SemaphoreType.DMA],
            input_output_aliases={0: 0} if carried else {},
            compiler_params=params(),
        )(*carried, *back)
    return result


def shards_of(*args):
    members = lax.axis_size("seq")
    rows, feat = args[0].shape
    chips = members // 2
    tiles = args[4].shape[0]
    if (
        members % 2 == 0
        and feat // HD % chips == 0
        and rows % 16 == 0
        and tiles <= META
        and tiles * members <= HD
    ):
        return by_heads(*args)
    return shards(*args)


def solution(mesh):
    return jax.shard_map(
        shards_of,
        mesh=mesh,
        in_specs=(
            P(("dp", "seq"), None),
            P(("dp", "seq"), None),
            P(("dp", "seq"), None),
            P("dp"),
            P(("dp", "seq"), None),
            P(("dp", "seq")),
        ),
        out_specs=P(("dp", "seq"), None),
        check_vma=False,
    )
```
